32 devices in a mesh: tx: 2 (over x), box: 16 (over z, y, core).
Axes of the slice: x: 2, y: 2, z: 4, core: 2. Of those that a mesh axis runs over, the one named last changes fastest.
Arguments:
- contrast_tangent: bfloat16 [16, 128], P('box', 'tx'), may hold values from -6 to 6
- incident: bfloat16 [64, 16, 128], P('tx', 'box'), may hold values from -6 to 6
- background: bfloat16 [16, 128], P('box'), may hold values from -3 to 3
- counts: int32 [16], P('box'), may hold values from 1 to 64, as said below
- box_mats: bfloat16 [16, 16384, 128], P('box'), may hold values from -0.046875 to 0.046875
- centers: float32 [3, 16], replicated, may hold values from -8 to 8
Outputs:
- hessian_product: float32 [16, 128], P('box', 'tx')
The draws below stay inside these ranges and needn't reach their ends.
Inputs may be any that keep to these rules, and one draw needn't show every extreme that they name: Each box's occupied voxels are the first counts slots of its 64; some box is full and some holds one voxel.
All inputs are finite; a program needn't handle non-finite values.
Results may differ from the reference program's by a relative error of at most 0.004.
Values may be sent and summed in bfloat16 or wider, within the bound.
No kernel may reach another device: no remote copies, remote signals or barrier semaphores. Data moves between devices by JAX's collectives and lax.ppermute only.
A program may use at most 64 MiB of HBM per device.

```python
import jax
import jax.numpy as jnp
from jax import lax

VB = 64
KT = 8192
TX = 64
NB = 16


def draw_counts(key, part):
    first_key = jax.random.fold_in(key, 11)
    second_key = jax.random.fold_in(key, 12)
    raw_draw = jax.random.randint(first_key, (NB,), 1, VB + 1)
    order = jax.random.permutation(second_key, NB)
    raw_draw = raw_draw.at[order[0]].set(VB).at[order[1]].set(1)
    return jnp.maximum(raw_draw * raw_draw // VB, 1).astype(jnp.int32)


def levels(key, shape, shards, least, top_value):
    level, own = 1.0, jax.random.fold_in(key, 6)
    for axis_at, shards_of in shards:
        draws = jnp.exp(jax.random.uniform(jax.random.fold_in(own, axis_at), (shards_of,), jnp.float32, least / len(shards), top_value / len(shards)))
        level = level * jnp.repeat(draws, shape[axis_at] // shards_of).reshape([-1 if axis == axis_at else 1 for axis in range(len(shape))])
    return level


def scatter_about(rng, shape, deviation, most, pieces=(), kind=jnp.bfloat16):
    gain = levels(rng, shape, pieces, -0.22, 0.18) if pieces else 1.0
    drawn = jax.random.normal(rng, shape, jnp.float32) * deviation * gain
    return jnp.minimum(jnp.maximum(drawn, -most), most).astype(kind)


def setup_inputs(seed: int = 0) -> dict:
    key_of = jax.random.split(jax.random.key(seed), 7)
    contrast_tangent = scatter_about(key_of[0], (NB, 2 * VB), 1.0, 6.0, ((0, 16), (1, 2)))
    incident = scatter_about(key_of[1], (TX, NB, 2 * VB), 1.0, 6.0, ((0, 2), (1, 16)))
    background = scatter_about(key_of[2], (NB, 2 * VB), 0.5, 3.0, ((0, 16),))
    counts = draw_counts(jax.random.fold_in(key_of[6], 71), 0)
    box_mats = scatter_about(key_of[4], (NB, 2 * KT, 2 * VB), (2 * KT) ** -0.5, 0.046875, ((0, 16),))
    centers = jnp.clip(jax.random.uniform(key_of[5], (3, NB), jnp.float32, -8.0, 8.0), -8.0, 8.0)
    return dict(contrast_tangent=contrast_tangent, incident=incident, background=background, counts=counts, box_mats=box_mats, centers=centers)


def directions(first_id, sample_count, total_count):
    sample_ids = first_id + jnp.arange(sample_count, dtype=jnp.int32)
    height = 1.0 - (2.0 * sample_ids.astype(jnp.float32) + 1.0) / total_count
    radial = jnp.sqrt(1.0 - height * height)
    turn_ids = sample_ids * 1597 % 4181
    azimuth = 2.0 * jnp.pi / 4181.0 * turn_ids.astype(jnp.float32)
    return (radial * jnp.cos(azimuth), radial * jnp.sin(azimuth), height)

def box_phases(centers, dirs):
    phases = jnp.pi * (centers[0][:, None] * dirs[0][None, :] + centers[1][:, None] * dirs[1][None, :] + centers[2][:, None] * dirs[2][None, :])
    return (jnp.cos(phases), jnp.sin(phases))

def times_complex(left, right):
    half = left.shape[-1] // 2
    left_re, left_im = (left[..., :half], left[..., half:])
    right_re, right_im = (right[..., :half], right[..., half:])
    return jnp.concatenate([left_re * right_re - left_im * right_im, left_re * right_im + left_im * right_re], -1)

def times_conj(left, right):
    half = left.shape[-1] // 2
    left_re, left_im = (left[..., :half], left[..., half:])
    right_re, right_im = (right[..., :half], right[..., half:])
    return jnp.concatenate([left_re * right_re + left_im * right_im, left_re * right_im - left_im * right_re], -1)

def far_apply(sources, box_mats, cosine, sine_part):
    samples = box_mats.shape[1] // 2

    def aggregate(top_field, inputs):
        source, matrix, cos_box, sin_box = inputs
        pattern = jnp.dot(source, matrix.T, preferred_element_type=jnp.float32).astype(jnp.bfloat16)
        pattern = lax.optimization_barrier(pattern).astype(jnp.float32)
        real_part = pattern[:, :samples]
        imag_part = pattern[:, samples:]
        top_re = top_field[0] + (cos_box * real_part - sin_box * imag_part)
        top_im = top_field[1] + (sin_box * real_part + cos_box * imag_part)
        return (jnp.stack([top_re, top_im]), None)
    start = jnp.zeros((2, sources.shape[1], samples), jnp.float32)
    top_field = lax.scan(aggregate, start, (sources, box_mats, cosine, sine_part))[0]

    def spread(inputs):
        matrix, cos_box, sin_box = inputs
        back_re = cos_box * top_field[0] + sin_box * top_field[1]
        back_im = cos_box * top_field[1] - sin_box * top_field[0]
        returned = jnp.concatenate([back_re, back_im], -1).astype(jnp.bfloat16)
        return jnp.dot(returned, matrix, preferred_element_type=jnp.float32)
    return lax.map(spread, (box_mats, cosine, sine_part))

def reference(contrast_tangent, incident, background, counts, box_mats, centers):
    dirs = directions(0, KT, KT)
    cosine, sine_part = box_phases(centers, dirs)
    live = (jnp.arange(VB, dtype=jnp.int32)[None, :] < counts[:, None]).astype(jnp.float32)
    live_mask = jnp.concatenate([live, live], -1)[:, None, :]
    incident_f = jnp.transpose(incident.astype(jnp.float32), (1, 0, 2))
    tangent = contrast_tangent.astype(jnp.float32)[:, None, :]
    backdrop = background.astype(jnp.float32)[:, None, :]
    source_one = (live_mask * times_complex(incident_f, tangent)).astype(jnp.bfloat16)
    scattered = far_apply(source_one, box_mats, cosine, sine_part)
    source_two = (source_one.astype(jnp.float32) + live_mask * times_complex(backdrop, scattered)).astype(jnp.bfloat16)
    adjoint = far_apply(source_two, box_mats, cosine, sine_part)
    weighted = (live_mask * times_conj(backdrop, adjoint)).astype(jnp.bfloat16)
    combined = adjoint + far_apply(weighted, box_mats, cosine, sine_part)
    return live_mask[:, 0, :] * lax.optimization_barrier(jnp.sum(times_conj(incident_f, combined), axis=1))
```

```python
import functools

import jax
import jax.numpy as jnp
from jax import lax
from jax.experimental import pallas as pl
from jax.experimental.pallas import tpu as pltpu
from jax.sharding import PartitionSpec as P


F32 = jnp.float32
BF16 = jnp.bfloat16
VMEM = pl.BlockSpec(memory_space=pltpu.VMEM)
CONTRACT_LAST = (((1,), (1,)), ((), ()))


def bits_below(total):
    assert total & (total - 1) == 0
    return [1 << k for k in range(total.bit_length() - 1)]


def directions(sample_ids, total_count):
    height = 1.0 - (2.0 * sample_ids.astype(F32) + 1.0) / total_count
    radial = jnp.sqrt(1.0 - height * height)
    turn_ids = sample_ids * 1597 % 4181
    azimuth = 2.0 * jnp.pi / 4181.0 * turn_ids.astype(F32)
    return (radial * jnp.cos(azimuth), radial * jnp.sin(azimuth), height)


def turned(values):
    return pltpu.roll(values, values.shape[-1] // 2, axis=values.ndim - 1)


def fill_kernel(group, *refs):
    pieces = refs[:group]
    cos_ref, sin_ref, packed_ref, coef_ref = refs[group : group + 4]
    rows_ref, source_ref, top_ref, send_ref, flat_ref = refs[group + 4 :]
    samples, width = pieces[0].shape[1:]
    planes, each = source_ref.shape[0] // group, source_ref.shape[1]
    for j in range(group):
        lanes = slice(j * width, (j + 1) * width)
        cos_j, sin_j = cos_ref[:, j : j + 1], sin_ref[:, j : j + 1]
        real, imag = pieces[j][0].astype(F32), pieces[j][1].astype(F32)
        rows_ref[:samples, lanes] = (cos_j * real - sin_j * imag).astype(BF16)
        rows_ref[samples:, lanes] = (sin_j * real + cos_j * imag).astype(BF16)
        for plane in range(planes):
            field = packed_ref[plane * group + j, :each, :].astype(F32)
            value = field * coef_ref[0, j : j + 1] + turned(field) * coef_ref[1, j : j + 1]
            value = value.astype(BF16)
            source_ref[plane * group + j] = value
            flat_ref[plane * each : (plane + 1) * each, lanes] = value
    top = lax.dot_general(flat_ref[...], rows_ref[...], CONTRACT_LAST, preferred_element_type=F32)
    top_ref[...] = top
    send_ref[...] = top.astype(BF16)


def back_kernel(group, top_ref, other_ref, rows_ref, part_ref, send_ref):
    planes, each = part_ref.shape[0] // group, part_ref.shape[1]
    width = part_ref.shape[2]
    returned = (top_ref[...] + other_ref[...].astype(F32)).astype(BF16)
    part = jnp.dot(returned, rows_ref[...], preferred_element_type=F32)
    for plane in range(planes):
        for j in range(group):
            block = part[plane * each : (plane + 1) * each, j * width : (j + 1) * width]
            part_ref[plane * group + j] = block
            send_ref[plane * group + j] = block.astype(BF16)


def next_kernel(group, bit, conj, *refs):
    if conj:
        part_ref, other_ref, coef_ref, rows_ref, top_ref, send_ref, flat_ref = refs
    else:
        part_ref, other_ref, coef_ref, first_ref, rows_ref, top_ref, send_ref, flat_ref = refs
    planes, each = part_ref.shape[0] // group, part_ref.shape[1]
    width = part_ref.shape[2]
    for plane in range(planes):
        for j in range(group):
            at = plane * group + j
            field = part_ref[at] + other_ref[at ^ bit].astype(F32)
            straight = field * coef_ref[2, j : j + 1]
            crossed = turned(field) * coef_ref[3, j : j + 1]
            if conj:
                value = straight - crossed
            else:
                value = first_ref[at].astype(F32) + (straight + crossed)
            flat_ref[plane * each : (plane + 1) * each, j * width : (j + 1) * width] = value.astype(BF16)
    top = lax.dot_general(flat_ref[...], rows_ref[...], CONTRACT_LAST, preferred_element_type=F32)
    top_ref[...] = top
    send_ref[...] = top.astype(BF16)


def last_kernel(group, top_ref, other_ref, rows_ref, part_ref, packed_ref, out_ref):
    planes, each = part_ref.shape[0] // group, part_ref.shape[1]
    width = part_ref.shape[2]
    returned = (top_ref[...] + other_ref[...].astype(F32)).astype(BF16)
    part = jnp.dot(returned, rows_ref[...], preferred_element_type=F32)
    low = lax.broadcasted_iota(jnp.int32, (1, width), 1) < width // 2
    for j in range(group):
        same = jnp.zeros((1, width), F32)
        cross = jnp.zeros((1, width), F32)
        for plane in range(planes):
            at = plane * group + j
            block = part[plane * each : (plane + 1) * each, j * width : (j + 1) * width] + part_ref[at]
            field = packed_ref[at, :each, :].astype(F32)
            same = same + jnp.sum(field * block, axis=0, keepdims=True)
            cross = cross + jnp.sum(field * turned(block), axis=0, keepdims=True)
        out_ref[j : j + 1] = jnp.where(low, same + turned(same), turned(cross) - cross)


def shards(contrast_tangent, incident, background, counts, box_mats, centers):
    tx_total, box_total = lax.axis_size("tx"), lax.axis_size("box")
    tx_id, box_id = lax.axis_index("tx"), lax.axis_index("box")
    group = max(box_total // 2, 1)
    halves = box_total // group
    members = tx_total * group
    each, width = incident.shape[0], incident.shape[2]
    half = width // 2
    count = tx_total * each
    matrix = box_mats[0]
    samples = matrix.shape[0] // 2
    piece = samples // members
    box_bits = bits_below(group)
    tx_bits = [bit * group for bit in bits_below(tx_total)]

    def swap(value, tx_bit, box_bit):
        pairs = [
            (t * box_total + b, (t ^ tx_bit) * box_total + (b ^ box_bit))
            for t in range(tx_total)
            for b in range(box_total)
        ]
        return lax.ppermute(value, ("tx", "box"), pairs)

    def swap_member(value, bit):
        return swap(value, bit // group, bit % group)

    planes = matrix.reshape(2, samples, width)

    def rows_for(other):
        chunk = tx_id * group + ((box_id ^ other) & (group - 1))
        return lax.dynamic_slice(planes, (0, chunk * piece, 0), (2, piece, width))

    pieces = [None] * group
    for other in reversed(range(group)):
        pieces[other] = swap(rows_for(other), 0, other) if other else rows_for(0)

    part_width = contrast_tangent.shape[1]
    own_tangent = lax.dynamic_update_slice(
        jnp.zeros((1, width), BF16), contrast_tangent, (0, tx_id * part_width)
    )
    live = (jnp.arange(half, dtype=jnp.int32)[None, :] < counts[:, None]).astype(F32)
    live_mask = jnp.concatenate([live, live], -1)
    packed = jnp.concatenate([incident[:, 0, :], own_tangent, background, live_mask.astype(BF16)], 0)
    packed = jnp.pad(packed, ((0, -packed.shape[0] % 16), (0, 0)))[None]
    for bit in box_bits + tx_bits:
        packed = jnp.concatenate([packed, swap_member(packed, bit)], 0)
    facts = packed.reshape(tx_total, group, -1, width)[:, :, each : each + 3].astype(F32)
    tangents, backdrops, lives = jnp.sum(facts[:, :, 0], axis=0), facts[0, :, 1], facts[0, :, 2]

    def factors(values):
        real, imag = values[:, :half], values[:, half:]
        return (
            lives * jnp.concatenate([real, real], -1),
            lives * jnp.concatenate([-imag, imag], -1),
        )

    coefs = jnp.stack(factors(tangents) + factors(backdrops))

    chosen = centers
    for bit in bits_below(box_total):
        paired = chosen.reshape(3, -1, 2, bit)
        chosen = jnp.where((box_id & bit) != 0, paired[:, :, ::-1], paired).reshape(3, box_total)
    chosen = chosen[:, :group]
    my_chunk = tx_id * group + (box_id & (group - 1))
    dirs = directions(my_chunk * piece + jnp.arange(piece, dtype=jnp.int32), samples)
    phases = jnp.pi * (
        dirs[0][:, None] * chosen[0][None, :]
        + dirs[1][:, None] * chosen[1][None, :]
        + dirs[2][:, None] * chosen[2][None, :]
    )
    cosine, sine_part = jnp.cos(phases), jnp.sin(phases)

    rows_type = jax.ShapeDtypeStruct((2 * piece, group * width), BF16)
    flat_type = pltpu.VMEM((count, group * width), BF16)
    top_types = (
        jax.ShapeDtypeStruct((count, 2 * piece), F32),
        jax.ShapeDtypeStruct((count, 2 * piece), BF16),
    )
    part_types = (
        jax.ShapeDtypeStruct((members, each, width), F32),
        jax.ShapeDtypeStruct((members, each, width), BF16),
    )
    source_type = jax.ShapeDtypeStruct((members, each, width), BF16)
    work = pl.CostEstimate(
        flops=2 * count * 2 * piece * group * width,
        bytes_accessed=2 * 2 * piece * group * width,
        transcendentals=0,
    )

    def call(kernel, outs, ins, scratch=()):
        return pl.pallas_call(
            kernel,
            out_shape=outs,
            in_specs=[VMEM] * len(ins),
            out_specs=jax.tree.map(lambda _: VMEM, outs),
            scratch_shapes=list(scratch),
            cost_estimate=work,
        )(*ins)

    def other_half(send):
        return swap(send, 0, group) if halves == 2 else jnp.zeros_like(send)

    sum_bits = tx_bits + box_bits
    if not sum_bits:
        sum_bits = [0]

    def summed(part, send):
        for bit in sum_bits[:-1]:
            arrived = swap_member(send, bit).reshape(-1, 2, bit, each, width)[:, ::-1]
            part = part + arrived.reshape(part.shape).astype(F32)
            send = part.astype(BF16)
        return part, swap_member(send, sum_bits[-1])

    rows, source_one, top, send = call(
        functools.partial(fill_kernel, group),
        (rows_type, source_type) + top_types,
        (*pieces, cosine, sine_part, packed, coefs),
        [flat_type],
    )
    back = functools.partial(back_kernel, group)
    part, send = call(back, part_types, (top, other_half(send), rows))
    part, arrived = summed(part, send)
    top, send = call(
        functools.partial(next_kernel, group, sum_bits[-1], False),
        top_types,
        (part, arrived, coefs, source_one, rows),
        [flat_type],
    )
    kept, send = call(back, part_types, (top, other_half(send), rows))
    part, arrived = summed(kept, send)
    top, send = call(
        functools.partial(next_kernel, group, sum_bits[-1], True),
        top_types,
        (part, arrived, coefs, rows),
        [flat_type],
    )
    product = call(
        functools.partial(last_kernel, group),
        jax.ShapeDtypeStruct((group, width), F32),
        (top, other_half(send), rows, kept, packed),
    )
    for bit in reversed(box_bits):
        product = product[:bit] + swap_member(product[bit:], bit)
    for bit in tx_bits:
        product = product + swap_member(product, bit)
    product = live_mask * product
    piece_width = width // tx_total
    return lax.dynamic_slice_in_dim(product, tx_id * piece_width, piece_width, 1)


def solution(mesh):
    placed = (
        P("box", "tx"),
        P("tx", "box", None),
        P("box", None),
        P("box"),
        P("box", None, None),
        P(),
    )
    return jax.shard_map(
        shards, mesh=mesh, in_specs=placed, out_specs=P("box", "tx"), check_vma=False
    )
```

```python
import functools

import jax
import jax.numpy as jnp
from jax import lax
from jax.experimental import pallas as pl
from jax.experimental.pallas import tpu as pltpu
from jax.sharding import PartitionSpec as P


F32 = jnp.float32
BF16 = jnp.bfloat16
VMEM = pl.BlockSpec(memory_space=pltpu.VMEM)
GRANT = 12 << 20
CONTRACT_LAST = (((1,), (1,)), ((), ()))


def bits_below(total):
    assert total & (total - 1) == 0
    return [1 << k for k in range(total.bit_length() - 1)]


def directions(sample_ids, total_count):
    height = 1.0 - (2.0 * sample_ids.astype(F32) + 1.0) / total_count
    radial = jnp.sqrt(1.0 - height * height)
    turn_ids = sample_ids * 1597 % 4181
    azimuth = 2.0 * jnp.pi / 4181.0 * turn_ids.astype(F32)
    return (radial * jnp.cos(azimuth), radial * jnp.sin(azimuth), height)


def turned(values):
    return pltpu.roll(values, values.shape[-1] // 2, axis=values.ndim - 1)


def fill_kernel(group, planes, each, *refs):
    pieces = refs[:group]
    cos_ref, sin_ref = refs[group : group + 2]
    packed = refs[group + 2 : group + 2 + group // 2]
    rows_ref, source_ref, coef_ref, top_ref, send_ref, flat_ref = refs[group + 2 + group // 2 :]
    samples, width = pieces[0].shape[1:]
    low = lax.broadcasted_iota(jnp.int32, (1, width), 1) < width // 2
    for j in range(group):
        lanes = slice(j * width, (j + 1) * width)
        cos_j, sin_j = cos_ref[:, j : j + 1], sin_ref[:, j : j + 1]
        real, imag = pieces[j][0].astype(F32), pieces[j][1].astype(F32)
        rows_ref[:samples, lanes] = (cos_j * real - sin_j * imag).astype(BF16)
        rows_ref[samples:, lanes] = (sin_j * real + cos_j * imag).astype(BF16)

        def fact(plane):
            return packed[j // 2][plane * 2 + j % 2, each:, :].astype(F32)

        def factors(value, live):
            other = turned(value)
            return jnp.where(low, value, other) * live, jnp.where(low, -other, value) * live

        facts = fact(0)
        live = facts[2:3]
        tangent = facts[0:1]
        for plane in range(1, planes):
            tangent = tangent + fact(plane)[0:1]
        straight, crossed = factors(tangent, live)
        if j % 2 == 0:
            kept = factors(facts[1:2], live)
            coef_ref[0, j // 2 : j // 2 + 1] = kept[0]
            coef_ref[1, j // 2 : j // 2 + 1] = kept[1]
        for plane in range(planes):
            field = packed[j // 2][plane * 2 + j % 2, :each, :].astype(F32)
            value = (field * straight + turned(field) * crossed).astype(BF16)
            if j % 2 == 0:
                source_ref[(plane * group + j) // 2] = value
            flat_ref[plane * each : (plane + 1) * each, lanes] = value
    top = lax.dot_general(flat_ref[...], rows_ref[...], CONTRACT_LAST, preferred_element_type=F32)
    top_ref[...] = top
    send_ref[...] = top.astype(BF16)


def back_kernel(group, top_ref, other_ref, rows_ref, part_ref, send_ref, *whole_ref):
    planes, each, width = part_ref.shape[0] * 2 // group, part_ref.shape[1], part_ref.shape[2]
    returned = (top_ref[...] + other_ref[...].astype(F32)).astype(BF16)
    part = jnp.dot(returned, rows_ref[...], preferred_element_type=F32)
    for plane in range(planes):
        for j in range(group):
            at = plane * group + j
            block = part[plane * each : (plane + 1) * each, j * width : (j + 1) * width]
            if j % 2:
                send_ref[at // 2] = block.astype(BF16)
            else:
                part_ref[at // 2] = block
            if whole_ref:
                whole_ref[0][at] = block


def source_kernel(group, bit, conj, part_ref, other_ref, coef_ref, *refs):
    out_ref = refs[-1]
    for at in range(part_ref.shape[0]):
        jj = at % (group // 2)
        field = part_ref[at] + other_ref[at ^ bit].astype(F32)
        straight = field * coef_ref[0, jj : jj + 1]
        crossed = turned(field) * coef_ref[1, jj : jj + 1]
        value = straight - crossed if conj else refs[0][at].astype(F32) + (straight + crossed)
        out_ref[at] = value.astype(BF16)


def top_kernel(group, even_ref, odd_ref, rows_ref, top_ref, send_ref, flat_ref):
    planes, each, width = even_ref.shape[0] * 2 // group, even_ref.shape[1], even_ref.shape[2]
    for plane in range(planes):
        for j in range(group):
            block = (odd_ref if j % 2 else even_ref)[(plane * group + j) // 2]
            flat_ref[plane * each : (plane + 1) * each, j * width : (j + 1) * width] = block
    top = lax.dot_general(flat_ref[...], rows_ref[...], CONTRACT_LAST, preferred_element_type=F32)
    top_ref[...] = top
    send_ref[...] = top.astype(BF16)


def last_kernel(group, planes, each, top_ref, other_ref, rows_ref, part_ref, *refs):
    packed, out_ref = refs[:-1], refs[-1]
    width = part_ref.shape[2]
    returned = (top_ref[...] + other_ref[...].astype(F32)).astype(BF16)
    part = jnp.dot(returned, rows_ref[...], preferred_element_type=F32)
    low = lax.broadcasted_iota(jnp.int32, (1, width), 1) < width // 2
    for j in range(group):
        same = jnp.zeros((1, width), F32)
        cross = jnp.zeros((1, width), F32)
        for plane in range(planes):
            block = part[plane * each : (plane + 1) * each, j * width : (j + 1) * width]
            block = block + part_ref[plane * group + j]
            field = packed[j // 2][plane * 2 + j % 2, :each, :].astype(F32)
            same = same + jnp.sum(field * block, axis=0, keepdims=True)
            cross = cross + jnp.sum(field * turned(block), axis=0, keepdims=True)
        out_ref[j : j + 1] = jnp.where(low, same + turned(same), turned(cross) - cross)


def shards(contrast_tangent, incident, background, counts, box_mats, centers):
    tx_total, box_total = lax.axis_size("tx"), lax.axis_size("box")
    tx_id, box_id = lax.axis_index("tx"), lax.axis_index("box")
    group = max(box_total // 2, 1)
    halves = box_total // group
    members = tx_total * group
    each, width = incident.shape[0], incident.shape[2]
    half = width // 2
    count = tx_total * each
    matrix = box_mats[0]
    samples = matrix.shape[0] // 2
    piece = samples // members
    box_bits = bits_below(group)
    tx_bits = [bit * group for bit in bits_below(tx_total)]

    def swap(value, tx_bit, box_bit):
        pairs = [
            (t * box_total + b, (t ^ tx_bit) * box_total + (b ^ box_bit))
            for t in range(tx_total)
            for b in range(box_total)
        ]
        return lax.ppermute(value, ("tx", "box"), pairs)

    def swap_member(value, bit):
        return swap(value, bit // group, bit % group)

    planes = matrix.reshape(2, samples, width)

    def rows_for(other):
        chunk = tx_id * group + ((box_id ^ other) & (group - 1))
        return lax.dynamic_slice(planes, (0, chunk * piece, 0), (2, piece, width))

    pieces = [None] * group
    for other in reversed(range(group)):
        pieces[other] = swap(rows_for(other), 0, other) if other else rows_for(0)

    part_width = contrast_tangent.shape[1]
    own_tangent = lax.dynamic_update_slice(
        jnp.zeros((1, width), BF16), contrast_tangent, (0, tx_id * part_width)
    )
    live = (jnp.arange(half, dtype=jnp.int32)[None, :] < counts[:, None]).astype(F32)
    live_mask = jnp.concatenate([live, live], -1)
    packed = jnp.concatenate([incident[:, 0, :], own_tangent, background, live_mask.astype(BF16)], 0)
    packed = jnp.pad(packed, ((0, -packed.shape[0] % 16), (0, 0)))[None]
    for bit in [1] + tx_bits:
        packed = jnp.concatenate([packed, swap_member(packed, bit)], 0)
    packed = [packed] + [swap_member(packed, other) for other in range(2, group, 2)]

    chosen = centers
    for bit in bits_below(box_total):
        paired = chosen.reshape(3, -1, 2, bit)
        chosen = jnp.where((box_id & bit) != 0, paired[:, :, ::-1], paired).reshape(3, box_total)
    chosen = chosen[:, :group]
    my_chunk = tx_id * group + (box_id & (group - 1))
    dirs = directions(my_chunk * piece + jnp.arange(piece, dtype=jnp.int32), samples)
    phases = jnp.pi * (
        dirs[0][:, None] * chosen[0][None, :]
        + dirs[1][:, None] * chosen[1][None, :]
        + dirs[2][:, None] * chosen[2][None, :]
    )
    cosine, sine_part = jnp.cos(phases), jnp.sin(phases)

    rows_type = jax.ShapeDtypeStruct((2 * piece, group * width), BF16)
    flat_type = pltpu.VMEM((count, group * width), BF16)
    top_types = (
        jax.ShapeDtypeStruct((count, 2 * piece), F32),
        jax.ShapeDtypeStruct((count, 2 * piece), BF16),
    )
    even_type = jax.ShapeDtypeStruct((members // 2, each, width), BF16)
    part_types = (jax.ShapeDtypeStruct(even_type.shape, F32), even_type)
    whole_type = jax.ShapeDtypeStruct((members, each, width), F32)
    coef_type = jax.ShapeDtypeStruct((2, group // 2, width), F32)
    work = pl.CostEstimate(
        flops=2 * count * 2 * piece * group * width,
        bytes_accessed=2 * 2 * piece * group * width,
        transcendentals=0,
    )

    def call(kernel, outs, ins, scratch=()):
        return pl.pallas_call(
            kernel,
            out_shape=outs,
            in_specs=[VMEM] * len(ins),
            out_specs=jax.tree.map(lambda _: VMEM, outs),
            scratch_shapes=list(scratch),
            compiler_params=pltpu.CompilerParams(vmem_limit_bytes=GRANT),
            cost_estimate=work,
        )(*ins)

    def other_half(send):
        return swap(send, 0, group) if halves == 2 else jnp.zeros_like(send)

    sum_bits = tx_bits + box_bits[1:]

    def summed(part, send):
        part = part + swap_member(send, 1).astype(F32)
        for bit in sum_bits[:-1]:
            arrived = swap_member(part.astype(BF16), bit)
            arrived = arrived.reshape(-1, 2, bit // 2, each, width)[:, ::-1]
            part = part + arrived.reshape(part.shape).astype(F32)
        return part, swap_member(part.astype(BF16), sum_bits[-1])

    def next_top(even):
        return call(
            functools.partial(top_kernel, group),
            top_types,
            (even, swap_member(even, 1), rows),
            [flat_type],
        )

    rows, source_one, coefs, top, send = call(
        functools.partial(fill_kernel, group, tx_total, each),
        (rows_type, even_type, coef_type) + top_types,
        (*pieces, cosine, sine_part, *packed),
        [flat_type],
    )
    back = functools.partial(back_kernel, group)
    source = functools.partial(source_kernel, group, sum_bits[-1] // 2)
    part, arrived = summed(*call(back, part_types, (top, other_half(send), rows)))
    source_two = call(
        functools.partial(source, False), even_type, (part, arrived, coefs, source_one)
    )
    top, send = next_top(source_two)
    part, send, kept = call(back, part_types + (whole_type,), (top, other_half(send), rows))
    part, arrived = summed(part, send)
    weighted = call(functools.partial(source, True), even_type, (part, arrived, coefs))
    top, send = next_top(weighted)
    product = call(
        functools.partial(last_kernel, group, tx_total, each),
        jax.ShapeDtypeStruct((group, width), F32),
        (top, other_half(send), rows, kept, *packed),
    )
    for bit in reversed(box_bits):
        product = product[:bit] + swap_member(product[bit:], bit)
    for bit in tx_bits:
        product = product + swap_member(product, bit)
    product = live_mask * product
    piece_width = width // tx_total
    return lax.dynamic_slice_in_dim(product, tx_id * piece_width, piece_width, 1)


def solution(mesh):
    placed = (
        P("box", "tx"),
        P("tx", "box", None),
        P("box", None),
        P("box"),
        P("box", None, None),
        P(),
    )
    return jax.shard_map(
        shards, mesh=mesh, in_specs=placed, out_specs=P("box", "tx"), check_vma=False
    )
```

```python
import functools

import jax
import jax.numpy as jnp
from jax import lax
from jax.experimental import pallas as pl
from jax.experimental.pallas import tpu as pltpu
from jax.sharding import PartitionSpec as P


F32 = jnp.float32
BF16 = jnp.bfloat16
VMEM = pl.BlockSpec(memory_space=pltpu.VMEM)
SMEM = pl.BlockSpec(memory_space=pltpu.SMEM)
GRANT = 12 << 20
SMALL = 2 << 20
CONTRACT_LAST = (((1,), (1,)), ((), ()))


def bits_below(total):
    assert total & (total - 1) == 0
    return [1 << k for k in range(total.bit_length() - 1)]


def turned(values):
    return pltpu.roll(values, values.shape[-1] // 2, axis=values.ndim - 1)


def slice_kernel(total, ids_ref, planes_ref, *refs):
    outs, sems = refs[:total], refs[total]
    size = outs[0].shape[1]
    copies = []
    for other in reversed(range(total)):
        chunk = ids_ref[0] * total + ((ids_ref[1] ^ other) & (total - 1))
        source = planes_ref.at[:, pl.ds(pl.multiple_of(chunk * size, size), size), :]
        copies.append(pltpu.make_async_copy(source, outs[other], sems.at[other]))
    for copy in copies:
        copy.start()
    for copy in copies:
        copy.wait()


def pack_kernel(tx_total, ids_ref, counts_ref, incident_ref, tangent_ref, backdrop_ref, out_ref):
    each, width = incident_ref.shape
    out_ref[0, :each, :] = incident_ref[...]
    shape = (out_ref.shape[1] - each, width)
    row = lax.broadcasted_iota(jnp.int32, shape, 0)
    lane = lax.broadcasted_iota(jnp.int32, shape, 1)
    tangent = jnp.concatenate([tangent_ref[...].astype(F32)] * tx_total, axis=-1)
    first = ids_ref[0] * (width // tx_total)
    mine = (lane >= first) & (lane < first + width // tx_total)
    half = width // 2
    slot = jnp.where(lane < half, lane, lane - half)
    facts = jnp.where((row == 0) & mine, jnp.broadcast_to(tangent, shape), 0.0)
    facts = jnp.where(row == 1, jnp.broadcast_to(backdrop_ref[...].astype(F32), shape), facts)
    facts = jnp.where(row == 2, jnp.where(slot < counts_ref[0], 1.0, 0.0), facts)
    out_ref[0, each:, :] = facts.astype(BF16)


def join_kernel(left_ref, right_ref, out_ref):
    at = left_ref.shape[0]
    out_ref[:at] = left_ref[...]
    out_ref[at:] = right_ref[...]


def phase_kernel(group, total, ids_ref, centers_ref, cos_ref, sin_ref, phase_ref):
    size = cos_ref.shape[0]
    chunk = ids_ref[0] * group + (ids_ref[1] & (group - 1))
    sample_ids = chunk * size + lax.broadcasted_iota(jnp.int32, (1, size), 1)
    height = 1.0 - (2.0 * sample_ids.astype(F32) + 1.0) / total
    radial = jnp.sqrt(1.0 - height * height)
    turn_ids = lax.rem(sample_ids * 1597, jnp.full_like(sample_ids, 4181))
    azimuth = 2.0 * jnp.pi / 4181.0 * turn_ids.astype(F32)
    along_x, along_y = radial * jnp.cos(azimuth), radial * jnp.sin(azimuth)
    for j in range(group):
        box = ids_ref[1] ^ j
        phase_ref[j : j + 1] = jnp.pi * (
            centers_ref[0, box] * along_x + centers_ref[1, box] * along_y + centers_ref[2, box] * height
        )
    cos_ref[...] = jnp.cos(phase_ref[...]).T
    sin_ref[...] = jnp.sin(phase_ref[...]).T


def fill_kernel(group, planes, each, *refs):
    pieces = refs[:group]
    cos_ref, sin_ref = refs[group : group + 2]
    packed = refs[group + 2 : group + 2 + group // 2]
    rows_ref, source_ref, coef_ref, top_ref, send_ref, flat_ref = refs[group + 2 + group // 2 :]
    samples, width = pieces[0].shape[1:]
    low = lax.broadcasted_iota(jnp.int32, (1, width), 1) < width // 2
    for j in range(group):
        lanes = slice(j * width, (j + 1) * width)
        cos_j, sin_j = cos_ref[:, j : j + 1], sin_ref[:, j : j + 1]
        real, imag = pieces[j][0].astype(F32), pieces[j][1].astype(F32)
        rows_ref[:samples, lanes] = (cos_j * real - sin_j * imag).astype(BF16)
        rows_ref[samples:, lanes] = (sin_j * real + cos_j * imag).astype(BF16)

        def fact(plane):
            return packed[j // 2][plane * 2 + j % 2, each:, :].astype(F32)

        def factors(value, live):
            other = turned(value)
            return jnp.where(low, value, other) * live, jnp.where(low, -other, value) * live

        facts = fact(0)
        live = facts[2:3]
        tangent = facts[0:1]
        for plane in range(1, planes):
            tangent = tangent + fact(plane)[0:1]
        straight, crossed = factors(tangent, live)
        if j % 2 == 0:
            kept = factors(facts[1:2], live)
            coef_ref[0, j // 2 : j // 2 + 1] = kept[0]
            coef_ref[1, j // 2 : j // 2 + 1] = kept[1]
        for plane in range(planes):
            field = packed[j // 2][plane * 2 + j % 2, :each, :].astype(F32)
            value = (field * straight + turned(field) * crossed).astype(BF16)
            if j % 2 == 0:
                source_ref[(plane * group + j) // 2] = value
            flat_ref[plane * each : (plane + 1) * each, lanes] = value
    top = lax.dot_general(flat_ref[...], rows_ref[...], CONTRACT_LAST, preferred_element_type=F32)
    top_ref[...] = top
    send_ref[...] = top.astype(BF16)


def back_kernel(group, top_ref, other_ref, rows_ref, part_ref, send_ref, *whole_ref):
    planes, each, width = part_ref.shape[0] * 2 // group, part_ref.shape[1], part_ref.shape[2]
    returned = (top_ref[...] + other_ref[...].astype(F32)).astype(BF16)
    part = jnp.dot(returned, rows_ref[...], preferred_element_type=F32)
    for plane in range(planes):
        for j in range(group):
            at = plane * group + j
            block = part[plane * each : (plane + 1) * each, j * width : (j + 1) * width]
            if j % 2:
                send_ref[at // 2] = block.astype(BF16)
            else:
                part_ref[at // 2] = block
            if whole_ref:
                whole_ref[0][at] = block


def source_kernel(group, bit, conj, part_ref, other_ref, coef_ref, *refs):
    out_ref = refs[-1]
    for at in range(part_ref.shape[0]):
        jj = at % (group // 2)
        field = part_ref[at] + other_ref[at ^ bit].astype(F32)
        straight = field * coef_ref[0, jj : jj + 1]
        crossed = turned(field) * coef_ref[1, jj : jj + 1]
        value = straight - crossed if conj else refs[0][at].astype(F32) + (straight + crossed)
        out_ref[at] = value.astype(BF16)


def top_kernel(group, even_ref, odd_ref, rows_ref, top_ref, send_ref, flat_ref):
    planes, each, width = even_ref.shape[0] * 2 // group, even_ref.shape[1], even_ref.shape[2]
    for plane in range(planes):
        for j in range(group):
            block = (odd_ref if j % 2 else even_ref)[(plane * group + j) // 2]
            flat_ref[plane * each : (plane + 1) * each, j * width : (j + 1) * width] = block
    top = lax.dot_general(flat_ref[...], rows_ref[...], CONTRACT_LAST, preferred_element_type=F32)
    top_ref[...] = top
    send_ref[...] = top.astype(BF16)


def last_kernel(group, planes, each, top_ref, other_ref, rows_ref, part_ref, *refs):
    packed, out_ref = refs[:-1], refs[-1]
    width = part_ref.shape[2]
    returned = (top_ref[...] + other_ref[...].astype(F32)).astype(BF16)
    part = jnp.dot(returned, rows_ref[...], preferred_element_type=F32)
    low = lax.broadcasted_iota(jnp.int32, (1, width), 1) < width // 2
    for j in range(group):
        same = jnp.zeros((1, width), F32)
        cross = jnp.zeros((1, width), F32)
        for plane in range(planes):
            block = part[plane * each : (plane + 1) * each, j * width : (j + 1) * width]
            block = block + part_ref[plane * group + j]
            field = packed[j // 2][plane * 2 + j % 2, :each, :].astype(F32)
            same = same + jnp.sum(field * block, axis=0, keepdims=True)
            cross = cross + jnp.sum(field * turned(block), axis=0, keepdims=True)
        out_ref[j : j + 1] = jnp.where(low, same + turned(same), turned(cross) - cross)


def shards(contrast_tangent, incident, background, counts, box_mats, centers):
    tx_total, box_total = lax.axis_size("tx"), lax.axis_size("box")
    tx_id, box_id = lax.axis_index("tx"), lax.axis_index("box")
    group = max(box_total // 2, 1)
    halves = box_total // group
    members = tx_total * group
    each, width = incident.shape[0], incident.shape[2]
    count = tx_total * each
    matrix = box_mats[0]
    samples = matrix.shape[0] // 2
    piece = samples // members
    box_bits = bits_below(group)
    tx_bits = [bit * group for bit in bits_below(tx_total)]

    def swap(value, tx_bit, box_bit):
        pairs = [
            (t * box_total + b, (t ^ tx_bit) * box_total + (b ^ box_bit))
            for t in range(tx_total)
            for b in range(box_total)
        ]
        return lax.ppermute(value, ("tx", "box"), pairs)

    def swap_member(value, bit):
        return swap(value, bit // group, bit % group)

    def call(kernel, outs, ins, scratch=(), specs=None, grant=GRANT, cost=None):
        return pl.pallas_call(
            kernel,
            out_shape=outs,
            in_specs=specs or [VMEM] * len(ins),
            out_specs=jax.tree.map(lambda _: VMEM, outs),
            scratch_shapes=list(scratch),
            compiler_params=pltpu.CompilerParams(vmem_limit_bytes=grant),
            cost_estimate=cost,
        )(*ins)

    ids = jnp.stack([tx_id, box_id]).astype(jnp.int32)
    planes = matrix.reshape(2, samples, width)
    pieces = call(
        functools.partial(slice_kernel, group),
        (jax.ShapeDtypeStruct((2, piece, width), BF16),) * group,
        (ids, planes),
        [pltpu.SemaphoreType.DMA((group,))],
        [SMEM, pl.BlockSpec(memory_space=pltpu.HBM)],
        SMALL,
    )
    pieces = [pieces[0]] + [swap(pieces[other], 0, other) for other in range(1, group)]

    rows_up = -(-(each + 3) // 16) * 16

    def joined(left, right):
        shape = (2 * left.shape[0],) + left.shape[1:]
        return call(join_kernel, jax.ShapeDtypeStruct(shape, BF16), (left, right), grant=SMALL)

    packed = call(
        functools.partial(pack_kernel, tx_total),
        jax.ShapeDtypeStruct((1, rows_up, width), BF16),
        (ids, counts, incident[:, 0, :], contrast_tangent, background),
        specs=[SMEM, SMEM, VMEM, VMEM, VMEM],
        grant=SMALL,
    )
    for bit in [1] + tx_bits:
        packed = joined(packed, swap_member(packed, bit))
    packed = [packed] + [swap_member(packed, other) for other in range(2, group, 2)]
    cosine, sine_part = call(
        functools.partial(phase_kernel, group, samples),
        (jax.ShapeDtypeStruct((piece, group), F32),) * 2,
        (ids, centers),
        [pltpu.VMEM((group, piece), F32)],
        [SMEM, SMEM],
        SMALL,
    )

    rows_type = jax.ShapeDtypeStruct((2 * piece, group * width), BF16)
    flat_type = pltpu.VMEM((count, group * width), BF16)
    top_types = (
        jax.ShapeDtypeStruct((count, 2 * piece), F32),
        jax.ShapeDtypeStruct((count, 2 * piece), BF16),
    )
    even_type = jax.ShapeDtypeStruct((members // 2, each, width), BF16)
    part_types = (jax.ShapeDtypeStruct(even_type.shape, F32), even_type)
    whole_type = jax.ShapeDtypeStruct((members, each, width), F32)
    coef_type = jax.ShapeDtypeStruct((2, group // 2, width), F32)
    work = pl.CostEstimate(
        flops=2 * count * 2 * piece * group * width,
        bytes_accessed=2 * 2 * piece * group * width,
        transcendentals=0,
    )

    def other_half(send):
        return swap(send, 0, group) if halves == 2 else jnp.zeros_like(send)

    sum_bits = tx_bits + box_bits[1:]

    def summed(part, send):
        part = part + swap_member(send, 1).astype(F32)
        for bit in sum_bits[:-1]:
            arrived = swap_member(part.astype(BF16), bit)
            arrived = arrived.reshape(-1, 2, bit // 2, each, width)[:, ::-1]
            part = part + arrived.reshape(part.shape).astype(F32)
        return part, swap_member(part.astype(BF16), sum_bits[-1])

    def next_top(even):
        return call(
            functools.partial(top_kernel, group),
            top_types,
            (even, swap_member(even, 1), rows),
            [flat_type],
            cost=work,
        )

    rows, source_one, coefs, top, send = call(
        functools.partial(fill_kernel, group, tx_total, each),
        (rows_type, even_type, coef_type) + top_types,
        (*pieces, cosine, sine_part, *packed),
        [flat_type],
        cost=work,
    )
    back = functools.partial(back_kernel, group)
    source = functools.partial(source_kernel, group, sum_bits[-1] // 2)
    part, arrived = summed(*call(back, part_types, (top, other_half(send), rows)))
    source_two = call(
        functools.partial(source, False), even_type, (part, arrived, coefs, source_one)
    )
    top, send = next_top(source_two)
    part, send, kept = call(back, part_types + (whole_type,), (top, other_half(send), rows))
    part, arrived = summed(part, send)
    weighted = call(functools.partial(source, True), even_type, (part, arrived, coefs))
    top, send = next_top(weighted)
    product = call(
        functools.partial(last_kernel, group, tx_total, each),
        jax.ShapeDtypeStruct((group, width), F32),
        (top, other_half(send), rows, kept, *packed),
    )
    for bit in reversed(box_bits):
        product = product[:bit] + swap_member(product[bit:], bit)
    for bit in tx_bits:
        product = product + swap_member(product, bit)
    live = (jnp.arange(width // 2, dtype=jnp.int32)[None, :] < counts[:, None]).astype(F32)
    product = jnp.concatenate([live, live], -1) * product
    piece_width = width // tx_total
    return lax.dynamic_slice_in_dim(product, tx_id * piece_width, piece_width, 1)


def solution(mesh):
    placed = (
        P("box", "tx"),
        P("tx", "box", None),
        P("box", None),
        P("box"),
        P("box", None, None),
        P(),
    )
    return jax.shard_map(
        shards, mesh=mesh, in_specs=placed, out_specs=P("box", "tx"), check_vma=False
    )
```

```python
import functools

import jax
import jax.numpy as jnp
from jax import lax
from jax.experimental import pallas as pl
from jax.experimental.pallas import tpu as pltpu
from jax.sharding import PartitionSpec as P


F32 = jnp.float32
BF16 = jnp.bfloat16
VMEM = pl.BlockSpec(memory_space=pltpu.VMEM)
SMEM = pl.BlockSpec(memory_space=pltpu.SMEM)
GRANT = 12 << 20
SMALL = 2 << 20
WHOLE = 60 << 20
CONTRACT_LAST = (((1,), (1,)), ((), ()))


def bits_below(total):
    assert total & (total - 1) == 0
    return [1 << k for k in range(total.bit_length() - 1)]


def turned(values):
    return pltpu.roll(values, values.shape[-1] // 2, axis=values.ndim - 1)


def slice_kernel(total, ids_ref, planes_ref, *refs):
    outs, sems = refs[:total], refs[total]
    size = outs[0].shape[1]
    copies = []
    for other in reversed(range(total)):
        chunk = ids_ref[0] * total + ((ids_ref[1] ^ other) & (total - 1))
        source = planes_ref.at[:, pl.ds(pl.multiple_of(chunk * size, size), size), :]
        copies.append(pltpu.make_async_copy(source, outs[other], sems.at[other]))
    for copy in copies:
        copy.start()
    for copy in copies:
        copy.wait()


def pack_kernel(tx_total, ids_ref, counts_ref, incident_ref, tangent_ref, backdrop_ref, out_ref):
    each, width = incident_ref.shape
    out_ref[0, :each, :] = incident_ref[...]
    shape = (out_ref.shape[1] - each, width)
    row = lax.broadcasted_iota(jnp.int32, shape, 0)
    lane = lax.broadcasted_iota(jnp.int32, shape, 1)
    tangent = jnp.concatenate([tangent_ref[...].astype(F32)] * tx_total, axis=-1)
    first = ids_ref[0] * (width // tx_total)
    mine = (lane >= first) & (lane < first + width // tx_total)
    half = width // 2
    slot = jnp.where(lane < half, lane, lane - half)
    facts = jnp.where((row == 0) & mine, jnp.broadcast_to(tangent, shape), 0.0)
    facts = jnp.where(row == 1, jnp.broadcast_to(backdrop_ref[...].astype(F32), shape), facts)
    facts = jnp.where(row == 2, jnp.where(slot < counts_ref[0], 1.0, 0.0), facts)
    out_ref[0, each:, :] = facts.astype(BF16)


def join_kernel(left_ref, right_ref, out_ref):
    at = left_ref.shape[0]
    out_ref[:at] = left_ref[...]
    out_ref[at:] = right_ref[...]


def phase_kernel(group, total, ids_ref, centers_ref, cos_ref, sin_ref, phase_ref):
    size = cos_ref.shape[0]
    chunk = ids_ref[0] * group + (ids_ref[1] & (group - 1))
    sample_ids = chunk * size + lax.broadcasted_iota(jnp.int32, (1, size), 1)
    height = 1.0 - (2.0 * sample_ids.astype(F32) + 1.0) / total
    radial = jnp.sqrt(1.0 - height * height)
    turn_ids = lax.rem(sample_ids * 1597, jnp.full_like(sample_ids, 4181))
    azimuth = 2.0 * jnp.pi / 4181.0 * turn_ids.astype(F32)
    along_x, along_y = radial * jnp.cos(azimuth), radial * jnp.sin(azimuth)
    for j in range(group):
        box = ids_ref[1] ^ j
        phase_ref[j : j + 1] = jnp.pi * (
            centers_ref[0, box] * along_x + centers_ref[1, box] * along_y + centers_ref[2, box] * height
        )
    cos_ref[...] = jnp.cos(phase_ref[...]).T
    sin_ref[...] = jnp.sin(phase_ref[...]).T


def turn_rows(rows_ref, piece_ref, cos_ref, sin_ref, j):
    samples, width = piece_ref.shape[1:]
    lanes = slice(j * width, (j + 1) * width)
    cos_j, sin_j = cos_ref[:, j : j + 1], sin_ref[:, j : j + 1]
    real, imag = piece_ref[0].astype(F32), piece_ref[1].astype(F32)
    rows_ref[:samples, lanes] = (cos_j * real - sin_j * imag).astype(BF16)
    rows_ref[samples:, lanes] = (sin_j * real + cos_j * imag).astype(BF16)


def fill_kernel(group, planes, each, *refs):
    pieces = refs[: group - 1]
    cos_ref, sin_ref = refs[group - 1 : group + 1]
    packed = refs[group + 1 : group + 1 + group // 2]
    rows_ref, source_ref, coef_ref, top_ref, late_ref, flat_ref = refs[group + 1 + group // 2 :]
    width = pieces[0].shape[2]
    low = lax.broadcasted_iota(jnp.int32, (1, width), 1) < width // 2
    for j in range(group):
        lanes = slice(j * width, (j + 1) * width)
        if j < group - 1:
            turn_rows(rows_ref, pieces[j], cos_ref, sin_ref, j)

        def fact(plane):
            return packed[j // 2][plane * 2 + j % 2, each:, :].astype(F32)

        def factors(value, live):
            other = turned(value)
            return jnp.where(low, value, other) * live, jnp.where(low, -other, value) * live

        facts = fact(0)
        live = facts[2:3]
        tangent = facts[0:1]
        for plane in range(1, planes):
            tangent = tangent + fact(plane)[0:1]
        straight, crossed = factors(tangent, live)
        if j % 2 == 0:
            kept = factors(facts[1:2], live)
            coef_ref[0, j // 2 : j // 2 + 1] = kept[0]
            coef_ref[1, j // 2 : j // 2 + 1] = kept[1]
        for plane in range(planes):
            field = packed[j // 2][plane * 2 + j % 2, :each, :].astype(F32)
            value = (field * straight + turned(field) * crossed).astype(BF16)
            if j % 2 == 0:
                source_ref[(plane * group + j) // 2] = value
            if j < group - 1:
                flat_ref[plane * each : (plane + 1) * each, lanes] = value
            else:
                late_ref[plane * each : (plane + 1) * each] = value
    ready = (group - 1) * width
    top_ref[...] = lax.dot_general(
        flat_ref[...], rows_ref[:, :ready], CONTRACT_LAST, preferred_element_type=F32
    )


def finish_kernel(group, piece_ref, cos_ref, sin_ref, late_ref, part_ref, _, rows_ref, top_ref, send_ref):
    turn_rows(rows_ref, piece_ref, cos_ref, sin_ref, group - 1)
    lanes = slice((group - 1) * piece_ref.shape[2], group * piece_ref.shape[2])
    top = part_ref[...] + lax.dot_general(
        late_ref[...], rows_ref[:, lanes], CONTRACT_LAST, preferred_element_type=F32
    )
    top_ref[...] = top
    send_ref[...] = top.astype(BF16)


def back_kernel(group, top_ref, other_ref, rows_ref, part_ref, send_ref, *whole_ref):
    planes, each, width = part_ref.shape[0] * 2 // group, part_ref.shape[1], part_ref.shape[2]
    returned = (top_ref[...] + other_ref[...].astype(F32)).astype(BF16)
    part = jnp.dot(returned, rows_ref[...], preferred_element_type=F32)
    for plane in range(planes):
        for j in range(group):
            at = plane * group + j
            block = part[plane * each : (plane + 1) * each, j * width : (j + 1) * width]
            if j % 2:
                send_ref[at // 2] = block.astype(BF16)
            else:
                part_ref[at // 2] = block
            if whole_ref:
                whole_ref[0][at] = block


def source_kernel(group, bit, conj, part_ref, other_ref, coef_ref, *refs):
    out_ref = refs[-1]
    for at in range(part_ref.shape[0]):
        jj = at % (group // 2)
        field = part_ref[at] + other_ref[at ^ bit].astype(F32)
        straight = field * coef_ref[0, jj : jj + 1]
        crossed = turned(field) * coef_ref[1, jj : jj + 1]
        value = straight - crossed if conj else refs[0][at].astype(F32) + (straight + crossed)
        out_ref[at] = value.astype(BF16)


def top_kernel(group, even_ref, odd_ref, rows_ref, top_ref, send_ref, flat_ref):
    planes, each, width = even_ref.shape[0] * 2 // group, even_ref.shape[1], even_ref.shape[2]
    for plane in range(planes):
        for j in range(group):
            block = (odd_ref if j % 2 else even_ref)[(plane * group + j) // 2]
            flat_ref[plane * each : (plane + 1) * each, j * width : (j + 1) * width] = block
    top = lax.dot_general(flat_ref[...], rows_ref[...], CONTRACT_LAST, preferred_element_type=F32)
    top_ref[...] = top
    send_ref[...] = top.astype(BF16)


def last_kernel(group, planes, each, top_ref, other_ref, rows_ref, part_ref, *refs):
    packed, out_ref = refs[:-1], refs[-1]
    width = part_ref.shape[2]
    returned = (top_ref[...] + other_ref[...].astype(F32)).astype(BF16)
    part = jnp.dot(returned, rows_ref[...], preferred_element_type=F32)
    low = lax.broadcasted_iota(jnp.int32, (1, width), 1) < width // 2
    for j in range(group):
        same = jnp.zeros((1, width), F32)
        cross = jnp.zeros((1, width), F32)
        for plane in range(planes):
            block = part[plane * each : (plane + 1) * each, j * width : (j + 1) * width]
            block = block + part_ref[plane * group + j]
            field = packed[j // 2][plane * 2 + j % 2, :each, :].astype(F32)
            same = same + jnp.sum(field * block, axis=0, keepdims=True)
            cross = cross + jnp.sum(field * turned(block), axis=0, keepdims=True)
        out_ref[j : j + 1] = jnp.where(low, same + turned(same), turned(cross) - cross)


def shards(contrast_tangent, incident, background, counts, box_mats, centers):
    tx_total, box_total = lax.axis_size("tx"), lax.axis_size("box")
    tx_id, box_id = lax.axis_index("tx"), lax.axis_index("box")
    group = max(box_total // 2, 1)
    halves = box_total // group
    members = tx_total * group
    each, width = incident.shape[0], incident.shape[2]
    count = tx_total * each
    matrix = box_mats[0]
    samples = matrix.shape[0] // 2
    piece = samples // members
    box_bits = bits_below(group)
    tx_bits = [bit * group for bit in bits_below(tx_total)]

    def swap(value, tx_bit, box_bit):
        pairs = [
            (t * box_total + b, (t ^ tx_bit) * box_total + (b ^ box_bit))
            for t in range(tx_total)
            for b in range(box_total)
        ]
        return lax.ppermute(value, ("tx", "box"), pairs)

    def swap_member(value, bit):
        return swap(value, bit // group, bit % group)

    def call(kernel, outs, ins, scratch=(), specs=None, grant=GRANT, cost=None, aliases={}):
        return pl.pallas_call(
            kernel,
            out_shape=outs,
            in_specs=specs or [VMEM] * len(ins),
            out_specs=jax.tree.map(lambda _: VMEM, outs),
            scratch_shapes=list(scratch),
            compiler_params=pltpu.CompilerParams(vmem_limit_bytes=grant),
            cost_estimate=cost,
            input_output_aliases=aliases,
        )(*ins)

    ids = jnp.stack([tx_id, box_id]).astype(jnp.int32)
    planes = matrix.reshape(2, samples, width)
    pieces = call(
        functools.partial(slice_kernel, group),
        (jax.ShapeDtypeStruct((2, piece, width), BF16),) * group,
        (ids, planes),
        [pltpu.SemaphoreType.DMA((group,))],
        [SMEM, pl.BlockSpec(memory_space=pl.ANY)],
        WHOLE,
    )
    order = sorted(range(2, group - 1), key=lambda o: (bin(o // 2).count("1"), o % 2, o))
    pieces = list(pieces)
    for other in order + [1]:
        pieces[other] = swap(pieces[other], 0, other)
    pieces[-1] = swap(pieces[-1], 0, group - 1)

    rows_up = -(-(each + 3) // 16) * 16
    held = lax.optimization_barrier((pieces[0], ids, counts, incident[:, 0, :], contrast_tangent, background))
    pieces[0] = held[0]

    def joined(left, right):
        shape = (2 * left.shape[0],) + left.shape[1:]
        return call(join_kernel, jax.ShapeDtypeStruct(shape, BF16), (left, right), grant=SMALL)

    packed = call(
        functools.partial(pack_kernel, tx_total),
        jax.ShapeDtypeStruct((1, rows_up, width), BF16),
        held[1:],
        specs=[SMEM, SMEM, VMEM, VMEM, VMEM],
        grant=SMALL,
    )
    for bit in [1] + tx_bits:
        packed = joined(packed, swap_member(packed, bit))
    packed = [packed] + [swap_member(packed, other) for other in range(2, group, 2)]
    cosine, sine_part = call(
        functools.partial(phase_kernel, group, samples),
        (jax.ShapeDtypeStruct((piece, group), F32),) * 2,
        (ids, centers),
        [pltpu.VMEM((group, piece), F32)],
        [SMEM, SMEM],
        SMALL,
    )

    rows_type = jax.ShapeDtypeStruct((2 * piece, group * width), BF16)
    flat_type = pltpu.VMEM((count, group * width), BF16)
    top_types = (
        jax.ShapeDtypeStruct((count, 2 * piece), F32),
        jax.ShapeDtypeStruct((count, 2 * piece), BF16),
    )
    even_type = jax.ShapeDtypeStruct((members // 2, each, width), BF16)
    part_types = (jax.ShapeDtypeStruct(even_type.shape, F32), even_type)
    whole_type = jax.ShapeDtypeStruct((members, each, width), F32)
    coef_type = jax.ShapeDtypeStruct((2, group // 2, width), F32)
    work = pl.CostEstimate(
        flops=2 * count * 2 * piece * group * width,
        bytes_accessed=2 * 2 * piece * group * width,
        transcendentals=0,
    )

    def other_half(send):
        return swap(send, 0, group) if halves == 2 else jnp.zeros_like(send)

    sum_bits = tx_bits + box_bits[1:]

    def summed(part, send):
        part = part + swap_member(send, 1).astype(F32)
        for bit in sum_bits[:-1]:
            arrived = swap_member(part.astype(BF16), bit)
            arrived = arrived.reshape(-1, 2, bit // 2, each, width)[:, ::-1]
            part = part + arrived.reshape(part.shape).astype(F32)
        return part, swap_member(part.astype(BF16), sum_bits[-1])

    def next_top(even):
        return call(
            functools.partial(top_kernel, group),
            top_types,
            (even, swap_member(even, 1), rows),
            [flat_type],
            cost=work,
        )

    rows, source_one, coefs, top, late = call(
        functools.partial(fill_kernel, group, tx_total, each),
        (rows_type, even_type, coef_type, top_types[0], jax.ShapeDtypeStruct((count, width), BF16)),
        (*pieces[:-1], cosine, sine_part, *packed),
        [pltpu.VMEM((count, (group - 1) * width), BF16)],
        cost=work,
    )
    rows, top, send = call(
        functools.partial(finish_kernel, group),
        (rows_type,) + top_types,
        (pieces[-1], cosine, sine_part, late, top, rows),
        aliases={5: 0},
    )
    back = functools.partial(back_kernel, group)
    source = functools.partial(source_kernel, group, sum_bits[-1] // 2)
    part, arrived = summed(*call(back, part_types, (top, other_half(send), rows)))
    source_two = call(
        functools.partial(source, False), even_type, (part, arrived, coefs, source_one)
    )
    top, send = next_top(source_two)
    part, send, kept = call(back, part_types + (whole_type,), (top, other_half(send), rows))
    part, arrived = summed(part, send)
    weighted = call(functools.partial(source, True), even_type, (part, arrived, coefs))
    top, send = next_top(weighted)
    product = call(
        functools.partial(last_kernel, group, tx_total, each),
        jax.ShapeDtypeStruct((group, width), F32),
        (top, other_half(send), rows, kept, *packed),
    )
    for bit in reversed(box_bits):
        product = product[:bit] + swap_member(product[bit:], bit)
    for bit in tx_bits:
        product = product + swap_member(product, bit)
    live = (jnp.arange(width // 2, dtype=jnp.int32)[None, :] < counts[:, None]).astype(F32)
    product = jnp.concatenate([live, live], -1) * product
    piece_width = width // tx_total
    return lax.dynamic_slice_in_dim(product, tx_id * piece_width, piece_width, 1)


def solution(mesh):
    placed = (
        P("box", "tx"),
        P("tx", "box", None),
        P("box", None),
        P("box"),
        P("box", None, None),
        P(),
    )
    return jax.shard_map(
        shards, mesh=mesh, in_specs=placed, out_specs=P("box", "tx"), check_vma=False
    )
```

```python
import functools

import jax
import jax.numpy as jnp
from jax import lax
from jax.experimental import pallas as pl
from jax.experimental.pallas import tpu as pltpu
from jax.sharding import PartitionSpec as P


F32 = jnp.float32
BF16 = jnp.bfloat16
VMEM = pl.BlockSpec(memory_space=pltpu.VMEM)
SMEM = pl.BlockSpec(memory_space=pltpu.SMEM)
GRANT = 12 << 20
SMALL = 2 << 20
WHOLE = 50 << 20
CONTRACT_LAST = (((1,), (1,)), ((), ()))


def bits_below(total):
    assert total & (total - 1) == 0
    return [1 << k for k in range(total.bit_length() - 1)]


def turned(values):
    return pltpu.roll(values, values.shape[-1] // 2, axis=values.ndim - 1)


def slice_kernel(total, planes_ref, *refs):
    outs, sems = refs[:total], refs[total]
    size = outs[0].shape[1]
    copies = []
    for other in reversed(range(total)):
        chunk = lax.axis_index("tx") * total + ((lax.axis_index("box") ^ other) & (total - 1))
        source = planes_ref.at[:, pl.ds(pl.multiple_of(chunk * size, size), size), :]
        copies.append(pltpu.make_async_copy(source, outs[other], sems.at[other]))
    for copy in copies:
        copy.start()
    for copy in copies:
        copy.wait()


def pack_kernel(tx_total, counts_ref, incident_ref, tangent_ref, backdrop_ref, out_ref):
    each, width = incident_ref.shape
    out_ref[0, :each, :] = incident_ref[...]
    shape = (out_ref.shape[1] - each, width)
    row = lax.broadcasted_iota(jnp.int32, shape, 0)
    lane = lax.broadcasted_iota(jnp.int32, shape, 1)
    tangent = jnp.concatenate([tangent_ref[...].astype(F32)] * tx_total, axis=-1)
    first = lax.axis_index("tx") * (width // tx_total)
    mine = (lane >= first) & (lane < first + width // tx_total)
    half = width // 2
    slot = jnp.where(lane < half, lane, lane - half)
    facts = jnp.where((row == 0) & mine, jnp.broadcast_to(tangent, shape), 0.0)
    facts = jnp.where(row == 1, jnp.broadcast_to(backdrop_ref[...].astype(F32), shape), facts)
    facts = jnp.where(row == 2, jnp.where(slot < counts_ref[0], 1.0, 0.0), facts)
    out_ref[0, each:, :] = facts.astype(BF16)


def join_kernel(left_ref, right_ref, out_ref):
    at = left_ref.shape[0]
    out_ref[:at] = left_ref[...]
    out_ref[at:] = right_ref[...]


def phase_kernel(group, total, centers_ref, cos_ref, sin_ref, phase_ref):
    size = cos_ref.shape[0]
    me = lax.axis_index("box")
    chunk = lax.axis_index("tx") * group + (me & (group - 1))
    sample_ids = chunk * size + lax.broadcasted_iota(jnp.int32, (1, size), 1)
    height = 1.0 - (2.0 * sample_ids.astype(F32) + 1.0) / total
    radial = jnp.sqrt(1.0 - height * height)
    turn_ids = lax.rem(sample_ids * 1597, jnp.full_like(sample_ids, 4181))
    azimuth = 2.0 * jnp.pi / 4181.0 * turn_ids.astype(F32)
    along_x, along_y = radial * jnp.cos(azimuth), radial * jnp.sin(azimuth)
    for j in range(group):
        box = me ^ j
        phase_ref[j : j + 1] = jnp.pi * (
            centers_ref[0, box] * along_x + centers_ref[1, box] * along_y + centers_ref[2, box] * height
        )
    cos_ref[...] = jnp.cos(phase_ref[...]).T
    sin_ref[...] = jnp.sin(phase_ref[...]).T


def turn_rows(rows_ref, piece_ref, cos_ref, sin_ref, j):
    samples, width = piece_ref.shape[1:]
    lanes = slice(j * width, (j + 1) * width)
    cos_j, sin_j = cos_ref[:, j : j + 1], sin_ref[:, j : j + 1]
    real, imag = piece_ref[0].astype(F32), piece_ref[1].astype(F32)
    rows_ref[:samples, lanes] = (cos_j * real - sin_j * imag).astype(BF16)
    rows_ref[samples:, lanes] = (sin_j * real + cos_j * imag).astype(BF16)


def fill_kernel(group, planes, each, *refs):
    pieces = refs[: group - 1]
    cos_ref, sin_ref = refs[group - 1 : group + 1]
    packed = refs[group + 1 : group + 1 + group // 2]
    rows_ref, source_ref, coef_ref, top_ref, late_ref, flat_ref = refs[group + 1 + group // 2 :]
    width = pieces[0].shape[2]
    low = lax.broadcasted_iota(jnp.int32, (1, width), 1) < width // 2
    for j in range(group):
        lanes = slice(j * width, (j + 1) * width)
        if j < group - 1:
            turn_rows(rows_ref, pieces[j], cos_ref, sin_ref, j)

        def fact(plane):
            return packed[j // 2][plane * 2 + j % 2, each:, :].astype(F32)

        def factors(value, live):
            other = turned(value)
            return jnp.where(low, value, other) * live, jnp.where(low, -other, value) * live

        facts = fact(0)
        live = facts[2:3]
        tangent = facts[0:1]
        for plane in range(1, planes):
            tangent = tangent + fact(plane)[0:1]
        straight, crossed = factors(tangent, live)
        if j % 2 == 0:
            kept = factors(facts[1:2], live)
            coef_ref[0, j // 2 : j // 2 + 1] = kept[0]
            coef_ref[1, j // 2 : j // 2 + 1] = kept[1]
        for plane in range(planes):
            field = packed[j // 2][plane * 2 + j % 2, :each, :].astype(F32)
            value = (field * straight + turned(field) * crossed).astype(BF16)
            if j % 2 == 0:
                source_ref[(plane * group + j) // 2] = value
            if j < group - 1:
                flat_ref[plane * each : (plane + 1) * each, lanes] = value
            else:
                late_ref[plane * each : (plane + 1) * each] = value
    ready = (group - 1) * width
    top_ref[...] = lax.dot_general(
        flat_ref[...], rows_ref[:, :ready], CONTRACT_LAST, preferred_element_type=F32
    )


def finish_kernel(group, piece_ref, cos_ref, sin_ref, late_ref, part_ref, _, rows_ref, top_ref, send_ref):
    turn_rows(rows_ref, piece_ref, cos_ref, sin_ref, group - 1)
    lanes = slice((group - 1) * piece_ref.shape[2], group * piece_ref.shape[2])
    top = part_ref[...] + lax.dot_general(
        late_ref[...], rows_ref[:, lanes], CONTRACT_LAST, preferred_element_type=F32
    )
    top_ref[...] = top
    send_ref[...] = top.astype(BF16)


def back_kernel(group, top_ref, other_ref, rows_ref, part_ref, send_ref, *whole_ref):
    planes, each, width = part_ref.shape[0] * 2 // group, part_ref.shape[1], part_ref.shape[2]
    returned = (top_ref[...] + other_ref[...].astype(F32)).astype(BF16)
    part = jnp.dot(returned, rows_ref[...], preferred_element_type=F32)
    for plane in range(planes):
        for j in range(group):
            at = plane * group + j
            block = part[plane * each : (plane + 1) * each, j * width : (j + 1) * width]
            if j % 2:
                send_ref[at // 2] = block.astype(BF16)
            else:
                part_ref[at // 2] = block
            if whole_ref:
                whole_ref[0][at] = block


def source_kernel(group, bit, conj, part_ref, other_ref, coef_ref, *refs):
    out_ref = refs[-1]
    for at in range(part_ref.shape[0]):
        jj = at % (group // 2)
        field = part_ref[at] + other_ref[at ^ bit].astype(F32)
        straight = field * coef_ref[0, jj : jj + 1]
        crossed = turned(field) * coef_ref[1, jj : jj + 1]
        value = straight - crossed if conj else refs[0][at].astype(F32) + (straight + crossed)
        out_ref[at] = value.astype(BF16)


def top_kernel(group, even_ref, odd_ref, rows_ref, top_ref, send_ref, flat_ref):
    planes, each, width = even_ref.shape[0] * 2 // group, even_ref.shape[1], even_ref.shape[2]
    for plane in range(planes):
        for j in range(group):
            block = (odd_ref if j % 2 else even_ref)[(plane * group + j) // 2]
            flat_ref[plane * each : (plane + 1) * each, j * width : (j + 1) * width] = block
    top = lax.dot_general(flat_ref[...], rows_ref[...], CONTRACT_LAST, preferred_element_type=F32)
    top_ref[...] = top
    send_ref[...] = top.astype(BF16)


def last_kernel(group, planes, each, top_ref, other_ref, rows_ref, part_ref, *refs):
    packed, out_ref = refs[:-1], refs[-1]
    width = part_ref.shape[2]
    returned = (top_ref[...] + other_ref[...].astype(F32)).astype(BF16)
    part = jnp.dot(returned, rows_ref[...], preferred_element_type=F32)
    low = lax.broadcasted_iota(jnp.int32, (1, width), 1) < width // 2
    for j in range(group):
        same = jnp.zeros((1, width), F32)
        cross = jnp.zeros((1, width), F32)
        for plane in range(planes):
            block = part[plane * each : (plane + 1) * each, j * width : (j + 1) * width]
            block = block + part_ref[plane * group + j]
            field = packed[j // 2][plane * 2 + j % 2, :each, :].astype(F32)
            same = same + jnp.sum(field * block, axis=0, keepdims=True)
            cross = cross + jnp.sum(field * turned(block), axis=0, keepdims=True)
        out_ref[j : j + 1] = jnp.where(low, same + turned(same), turned(cross) - cross)


def shards(contrast_tangent, incident, background, counts, box_mats, centers):
    tx_total, box_total = lax.axis_size("tx"), lax.axis_size("box")
    tx_id = lax.axis_index("tx")
    group = max(box_total // 2, 1)
    halves = box_total // group
    members = tx_total * group
    each, width = incident.shape[0], incident.shape[2]
    count = tx_total * each
    matrix = box_mats[0]
    samples = matrix.shape[0] // 2
    piece = samples // members
    box_bits = bits_below(group)
    tx_bits = [bit * group for bit in bits_below(tx_total)]

    def swap(value, tx_bit, box_bit):
        pairs = [
            (t * box_total + b, (t ^ tx_bit) * box_total + (b ^ box_bit))
            for t in range(tx_total)
            for b in range(box_total)
        ]
        return lax.ppermute(value, ("tx", "box"), pairs)

    def swap_member(value, bit):
        return swap(value, bit // group, bit % group)

    def call(kernel, outs, ins, scratch=(), specs=None, grant=GRANT, cost=None, aliases={}):
        return pl.pallas_call(
            kernel,
            out_shape=outs,
            in_specs=specs or [VMEM] * len(ins),
            out_specs=jax.tree.map(lambda _: VMEM, outs),
            scratch_shapes=list(scratch),
            compiler_params=pltpu.CompilerParams(vmem_limit_bytes=grant),
            cost_estimate=cost,
            input_output_aliases=aliases,
        )(*ins)

    planes = matrix.reshape(2, samples, width)
    pieces = call(
        functools.partial(slice_kernel, group),
        (jax.ShapeDtypeStruct((2, piece, width), BF16),) * group,
        (planes,),
        [pltpu.SemaphoreType.DMA((group,))],
        [pl.BlockSpec(memory_space=pl.ANY)],
        WHOLE,
    )
    order = sorted(range(2, group - 1), key=lambda o: (bin(o // 2).count("1"), o % 2, o))
    pieces = list(pieces)
    for other in order + [1]:
        pieces[other] = swap(pieces[other], 0, other)
    pieces[-1] = swap(pieces[-1], 0, group - 1)

    rows_up = -(-(each + 3) // 16) * 16
    held = lax.optimization_barrier((pieces[0], counts, incident[:, 0, :], contrast_tangent, background))
    pieces[0] = held[0]

    def joined(left, right):
        shape = (2 * left.shape[0],) + left.shape[1:]
        return call(join_kernel, jax.ShapeDtypeStruct(shape, BF16), (left, right), grant=SMALL)

    packed = call(
        functools.partial(pack_kernel, tx_total),
        jax.ShapeDtypeStruct((1, rows_up, width), BF16),
        held[1:],
        specs=[SMEM, VMEM, VMEM, VMEM],
        grant=SMALL,
    )
    for bit in [1] + tx_bits:
        packed = joined(packed, swap_member(packed, bit))
    packed = [packed] + [swap_member(packed, other) for other in range(2, group, 2)]
    cosine, sine_part = call(
        functools.partial(phase_kernel, group, samples),
        (jax.ShapeDtypeStruct((piece, group), F32),) * 2,
        (centers,),
        [pltpu.VMEM((group, piece), F32)],
        [SMEM],
        SMALL,
    )

    rows_type = jax.ShapeDtypeStruct((2 * piece, group * width), BF16)
    flat_type = pltpu.VMEM((count, group * width), BF16)
    top_types = (
        jax.ShapeDtypeStruct((count, 2 * piece), F32),
        jax.ShapeDtypeStruct((count, 2 * piece), BF16),
    )
    even_type = jax.ShapeDtypeStruct((members // 2, each, width), BF16)
    part_types = (jax.ShapeDtypeStruct(even_type.shape, F32), even_type)
    whole_type = jax.ShapeDtypeStruct((members, each, width), F32)
    coef_type = jax.ShapeDtypeStruct((2, group // 2, width), F32)
    work = pl.CostEstimate(
        flops=2 * count * 2 * piece * group * width,
        bytes_accessed=2 * 2 * piece * group * width,
        transcendentals=0,
    )

    def other_half(send):
        return swap(send, 0, group) if halves == 2 else jnp.zeros_like(send)

    sum_bits = tx_bits + box_bits[1:]

    def summed(part, send):
        part = part + swap_member(send, 1).astype(F32)
        for bit in sum_bits[:-1]:
            arrived = swap_member(part.astype(BF16), bit)
            arrived = arrived.reshape(-1, 2, bit // 2, each, width)[:, ::-1]
            part = part + arrived.reshape(part.shape).astype(F32)
        return part, swap_member(part.astype(BF16), sum_bits[-1])

    def next_top(even):
        return call(
            functools.partial(top_kernel, group),
            top_types,
            (even, swap_member(even, 1), rows),
            [flat_type],
            cost=work,
        )

    rows, source_one, coefs, top, late = call(
        functools.partial(fill_kernel, group, tx_total, each),
        (rows_type, even_type, coef_type, top_types[0], jax.ShapeDtypeStruct((count, width), BF16)),
        (*pieces[:-1], cosine, sine_part, *packed),
        [pltpu.VMEM((count, (group - 1) * width), BF16)],
        cost=work,
    )
    rows, top, send = call(
        functools.partial(finish_kernel, group),
        (rows_type,) + top_types,
        (pieces[-1], cosine, sine_part, late, top, rows),
        aliases={5: 0},
    )
    back = functools.partial(back_kernel, group)
    source = functools.partial(source_kernel, group, sum_bits[-1] // 2)
    part, arrived = summed(*call(back, part_types, (top, other_half(send), rows)))
    source_two = call(
        functools.partial(source, False), even_type, (part, arrived, coefs, source_one)
    )
    top, send = next_top(source_two)
    part, send, kept = call(back, part_types + (whole_type,), (top, other_half(send), rows))
    part, arrived = summed(part, send)
    weighted = call(functools.partial(source, True), even_type, (part, arrived, coefs))
    top, send = next_top(weighted)
    product = call(
        functools.partial(last_kernel, group, tx_total, each),
        jax.ShapeDtypeStruct((group, width), F32),
        (top, other_half(send), rows, kept, *packed),
    )
    for bit in reversed(box_bits):
        product = product[:bit] + swap_member(product[bit:], bit)
    for bit in tx_bits:
        product = product + swap_member(product, bit)
    live = (jnp.arange(width // 2, dtype=jnp.int32)[None, :] < counts[:, None]).astype(F32)
    product = jnp.concatenate([live, live], -1) * product
    piece_width = width // tx_total
    return lax.dynamic_slice_in_dim(product, tx_id * piece_width, piece_width, 1)


def solution(mesh):
    placed = (
        P("box", "tx"),
        P("tx", "box", None),
        P("box", None),
        P("box"),
        P("box", None, None),
        P(),
    )
    return jax.shard_map(
        shards, mesh=mesh, in_specs=placed, out_specs=P("box", "tx"), check_vma=False
    )
```
